32 devices in a mesh: rows: 8 (over y, x, core), grp: 4 (over z).
Axes of the slice: x: 2, y: 2, z: 4, core: 2. Of those that a mesh axis runs over, the one named last changes fastest.
Arguments:
- date_keys: int32 [262144], P(('rows', 'grp')), may hold values from 0 to 2559
- product_keys: int32 [262144], P(('rows', 'grp')), may hold values from 0 to 16255
- quantity: float32 [262144], P(('rows', 'grp')), may hold values from 0.01 to 10
- date_flags: int32 [2560], P('rows'), may hold values 0 or 1
- category: int32 [16256], P('rows'), may hold values from 0 to 999
- unit_price: float32 [16256], P('rows'), may hold values from 0.5 to 4
- unit_cost: float32 [16256], P('rows'), may hold values from 0.25 to 2
Outputs:
- revenue_by_category: float32 [1000], replicated
- profit_by_category: float32 [1000], replicated
The draws below stay inside these ranges and needn't reach their ends.
All inputs are finite; a program needn't handle non-finite values. No bound on the sum of `date_flags` on one device may be relied on, other than what follows from the above.
Results may differ from the reference program's by a relative error of at most 0.00005.
Values sent between devices are 32-bit elements; how exact they have to be, the bound alone decides.
A program may use at most 192 MiB of HBM per device.

```python
import math
import jax
import jax.numpy as jnp
import numpy as np

CATS = 1000
DATES = 2560
PRODUCTS = 16256
FACTS = 262144


def with_ends(entries, key, smallest, top_value):
    longest = entries.shape.index(max(entries.shape))
    spots = []
    for shift in (0, 1):
        where = [jax.random.randint(jax.random.fold_in(key, axis), (), 0, length) for axis, length in enumerate(entries.shape)]
        where[longest] = (where[longest] + shift) % entries.shape[longest]
        spots.append(tuple(where))
    return entries.at[spots[0]].set(smallest).at[spots[1]].set(top_value)


def shard_levels(key, dims, pieces, least, high):
    def one(axis_at, blocks):
        steps = jax.random.uniform(jax.random.fold_in(jax.random.fold_in(key, 6), axis_at), (blocks,), jnp.float32, least / len(pieces), high / len(pieces))
        return jnp.repeat(jnp.exp(steps), dims[axis_at] // blocks).reshape((-1,) + (1,) * (len(dims) - axis_at - 1))

    factor_of = one(*pieces[0])
    for cut in pieces[1:]:
        factor_of = factor_of * one(*cut)
    return factor_of


def rank_table(amount, lean):
    loads = [(1 << 20) // math.isqrt(standing ** lean) + 1 for standing in range(1, amount + 1)]
    deviation = 1 + sum(loads) // (1 << 30)
    return np.cumsum(np.array([max(1, weight // deviation) for weight in loads]))


def skewed_ids(own_key, shape, count, skew):
    table = rank_table(count, skew)
    pick = jax.random.randint(jax.random.fold_in(own_key, 1), shape, 0, int(table[count - 1]))
    grade = jnp.searchsorted(jnp.asarray(table, jnp.int32), pick, side="right")
    return jax.random.permutation(jax.random.fold_in(own_key, 2), count)[grade].astype(jnp.int32)


def setup_inputs(seed: int = 0) -> dict:
    key_of = jax.random.split(jax.random.key(seed), 8)
    return {
        "date_keys": with_ends(jax.random.randint(key_of[0], (FACTS,), 0, DATES), jax.random.fold_in(key_of[0], 1), 0, DATES - 1).astype(jnp.int32),
        "product_keys": with_ends(skewed_ids(key_of[1], (FACTS,), PRODUCTS, 1), jax.random.fold_in(key_of[1], 3), 0, PRODUCTS - 1).astype(jnp.int32),
        "quantity": jnp.clip(jnp.exp(math.log(10.0) - 6.9077553 * jax.random.uniform(key_of[2], (FACTS,), jnp.float32) ** shard_levels(key_of[2], (FACTS,), ((0, 32),), -0.2, 0.2)), 0.01, 10.0),
        "date_flags": with_ends((jax.random.randint(key_of[3], (DATES,), 0, 2) < 1).astype(jnp.int32), jax.random.fold_in(key_of[3], 1), 0, 1),
        "category": with_ends(jax.random.randint(key_of[4], (PRODUCTS,), 0, CATS), jax.random.fold_in(key_of[4], 1), 0, CATS - 1).astype(jnp.int32),
        "unit_price": jnp.clip(jnp.exp(math.log(4.0) - 2.0794415 * jax.random.uniform(key_of[5], (PRODUCTS,), jnp.float32) ** shard_levels(key_of[5], (PRODUCTS,), ((0, 8),), -0.2, 0.2)), 0.5, 4.0),
        "unit_cost": jnp.clip(jnp.exp(math.log(2.0) - 2.0794415 * jax.random.uniform(key_of[6], (PRODUCTS,), jnp.float32) ** shard_levels(key_of[6], (PRODUCTS,), ((0, 8),), -0.2, 0.2)), 0.25, 2.0),
    }


def reference(date_keys, product_keys, quantity, date_flags, category, unit_price, unit_cost):
    passed = date_flags[date_keys]
    kept_amount = jnp.where(passed == 1, quantity, jnp.zeros_like(quantity))
    fact_price = unit_price[product_keys]
    fact_cost = unit_cost[product_keys]
    fact_category = category[product_keys]
    revenue = jax.ops.segment_sum(kept_amount * fact_price, fact_category, num_segments=CATS)
    profit = jax.ops.segment_sum(kept_amount * (fact_price - fact_cost), fact_category, num_segments=CATS)
    factor = CATS / FACTS
    return revenue * factor, profit * factor
```

```python
import functools

import jax
import jax.numpy as jnp
from jax import lax
from jax.experimental import pallas as pl
from jax.experimental.pallas import tpu as pltpu
from jax.sharding import PartitionSpec as P

CATS = 1000
LANES = 128
MESH = pl.DeviceIdType.MESH
NT = (((1,), (1,)), ((), ()))
SPLITS = 3


def cdiv(a, b):
    return (a + b - 1) // b


def split_bf16(value):
    parts = []
    for _ in range(SPLITS):
        part = value.astype(jnp.bfloat16).astype(jnp.float32)
        parts.append(part)
        value = value - part
    return parts


def divmod_const(keys, size, count):
    block = jnp.zeros_like(keys)
    for step in range(1, count):
        block = block + jnp.where(keys >= step * size, 1, 0)
    return block, keys - block * size


def row(ref, index):
    return ref[pl.ds(index, 1), :]


def kernel(
    rows,
    grps,
    flag_shard,
    shard,
    factor,
    flag_ref,
    table_ref,
    date_ref,
    product_ref,
    quantity_ref,
    out_ref,
    flags,
    tables,
    date_row,
    date_word,
    date_bit,
    key_hi,
    key_lo,
    word,
    kept,
    hist,
    values,
    cat_hi,
    cat_lo,
    grp_sums,
    row_sums,
    send_flag,
    recv_flag,
    send_table,
    recv_table,
    send_grp,
    recv_grp,
    send_row,
    recv_row,
):
    me = lax.axis_index("rows")
    mine = lax.axis_index("grp")
    flag_rows = flag_ref.shape[0]
    table_rows = table_ref.shape[0] // 3
    fact_rows = date_ref.shape[0]
    all_flag_rows = rows * flag_rows
    all_rows = rows * table_rows
    hi_cats = cdiv(CATS, LANES)

    barrier = pltpu.get_barrier_semaphore()
    for step in range(1, rows):
        pl.semaphore_signal(
            barrier, inc=1, device_id=(lax.rem(me + step, rows), mine), device_id_type=MESH
        )
    for step in range(1, grps):
        pl.semaphore_signal(
            barrier, inc=1, device_id=(me, lax.rem(mine + step, grps)), device_id_type=MESH
        )
    pl.semaphore_wait(barrier, rows + grps - 2)

    def to_rows(source, target, send, recv):
        copies = []
        for step in range(1, rows):
            copy = pltpu.make_async_remote_copy(
                src_ref=source,
                dst_ref=target,
                send_sem=send.at[step],
                recv_sem=recv.at[step],
                device_id=(lax.rem(me + step, rows), mine),
                device_id_type=MESH,
            )
            copy.start()
            copies.append(copy)
        return copies

    flag_copies = to_rows(flag_ref, flags.at[me], send_flag, recv_flag)
    table_copies = to_rows(table_ref, tables.at[me], send_table, recv_table)
    flags[pl.ds(me, 1)] = flag_ref[...][None]
    tables[pl.ds(me, 1)] = table_ref[...][None]

    block, inside = divmod_const(date_ref[...], flag_shard, rows)
    date_row[...] = block * flag_rows + inside // LANES
    date_word[...] = (inside % LANES) // 8
    date_bit[...] = inside % 8
    block, inside = divmod_const(product_ref[...], shard, rows)
    key_hi[...] = block * table_rows + inside // LANES
    key_lo[...] = inside % LANES

    for copy in flag_copies:
        copy.wait()

    lane = lax.broadcasted_iota(jnp.int32, (16, LANES), 1)
    place = lax.broadcasted_iota(jnp.int32, (16, LANES), 0)
    weight = jnp.where(
        lane // 8 == place, jnp.left_shift(jnp.ones_like(lane), lane % 8), 0
    ).astype(jnp.float32).astype(jnp.bfloat16)
    words = lax.dot_general(
        weight,
        flags[...].reshape(all_flag_rows, LANES).astype(jnp.bfloat16),
        NT,
        preferred_element_type=jnp.float32,
    ).astype(jnp.bfloat16)
    flag_iota = lax.broadcasted_iota(jnp.int32, (all_flag_rows, LANES), 0)

    @pl.loop(0, fact_rows // 8)
    def _(chunk):
        base = chunk * 8
        onehot = jnp.concatenate(
            [
                jnp.where(flag_iota == row(date_row, base + i), 1.0, 0.0).astype(jnp.bfloat16)
                for i in range(8)
            ],
            axis=1,
        )
        found = jnp.dot(words, onehot, preferred_element_type=jnp.float32)
        for i in range(8):
            piece = found[:, i * LANES : (i + 1) * LANES]
            picked = jnp.where(place == row(date_word, base + i), piece, 0.0)
            word[pl.ds(base + i, 1), :] = jnp.sum(picked, axis=0, keepdims=True)

    passed = jnp.right_shift(word[...].astype(jnp.int32), date_bit[...]) & 1
    for s, part in enumerate(split_bf16(jnp.where(passed == 1, quantity_ref[...], 0.0))):
        kept[s] = part

    square = lax.broadcasted_iota(jnp.int32, (LANES, LANES), 0)
    hist[...] = jnp.zeros_like(hist)

    @pl.loop(0, fact_rows // 8)
    def _(chunk):
        base = chunk * 8
        amounts = [[] for _ in range(SPLITS)]
        for i in range(8):
            mask = square == row(key_lo, base + i)
            for s in range(SPLITS):
                amount = kept[s, pl.ds(base + i, 1), :]
                amounts[s].append(jnp.where(mask, amount, 0.0).astype(jnp.bfloat16))
        amounts = [jnp.concatenate(parts, axis=1) for parts in amounts]

        def add(first, count):
            spot = lax.broadcasted_iota(jnp.int32, (count, LANES), 0) + first
            onehot = jnp.concatenate(
                [
                    jnp.where(spot == row(key_hi, base + i), 1.0, 0.0).astype(jnp.bfloat16)
                    for i in range(8)
                ],
                axis=1,
            )
            total = hist[pl.ds(first, count), :]
            for s in range(SPLITS):
                total = total + lax.dot_general(
                    onehot, amounts[s], NT, preferred_element_type=jnp.float32
                )
            hist[pl.ds(first, count), :] = total

        for first in range(0, all_rows, LANES):
            add(first, min(LANES, all_rows - first))

    for copy in table_copies:
        copy.wait()

    @pl.loop(0, rows)
    def _(r):
        amount = hist[pl.ds(pl.multiple_of(r * table_rows, table_rows), table_rows), :]
        spot = pl.ds(pl.multiple_of(r * table_rows, table_rows), table_rows)
        table = tables[r]
        price = table[:table_rows]
        margin = table[table_rows : 2 * table_rows]
        category = table[2 * table_rows :].astype(jnp.int32)
        cat_hi[spot, :] = category // LANES
        cat_lo[spot, :] = category % LANES
        for s, part in enumerate(split_bf16(amount * price)):
            values[2 * s, spot, :] = part
        for s, part in enumerate(split_bf16(amount * margin)):
            values[2 * s + 1, spot, :] = part

    cat_iota = lax.broadcasted_iota(jnp.int32, (hi_cats, LANES), 0)

    def add_products(chunk, running):
        base = chunk * 8
        lefts, rights = [], []
        for i in range(8):
            mask = cat_iota == row(cat_hi, base + i)
            lefts.append(
                jnp.concatenate(
                    [
                        jnp.where(mask, values[v, pl.ds(base + i, 1), :], 0.0)
                        for v in range(2 * SPLITS)
                    ],
                    axis=0,
                ).astype(jnp.bfloat16)
            )
            rights.append(
                jnp.where(square == row(cat_lo, base + i), 1.0, 0.0).astype(jnp.bfloat16)
            )
        return running + lax.dot_general(
            jnp.concatenate(lefts, axis=1),
            jnp.concatenate(rights, axis=1),
            NT,
            preferred_element_type=jnp.float32,
        )

    summed = lax.fori_loop(
        0,
        all_rows // 8,
        add_products,
        jnp.zeros((2 * SPLITS * hi_cats, LANES), jnp.float32),
    )
    size = 2 * hi_cats
    partial = summed[:size]
    for s in range(1, SPLITS):
        partial = partial + summed[s * size : (s + 1) * size]

    grp_sums[pl.ds(mine, 1)] = partial[None]
    copies = []
    for step in range(1, grps):
        copy = pltpu.make_async_remote_copy(
            src_ref=grp_sums.at[mine],
            dst_ref=grp_sums.at[mine],
            send_sem=send_grp.at[step],
            recv_sem=recv_grp.at[step],
            device_id=(me, lax.rem(mine + step, grps)),
            device_id_type=MESH,
        )
        copy.start()
        copies.append(copy)
    for copy in copies:
        copy.wait()
    total = grp_sums[0]
    for g in range(1, grps):
        total = total + grp_sums[g]

    row_sums[pl.ds(me, 1)] = total[None]
    for copy in to_rows(row_sums.at[me], row_sums.at[me], send_row, recv_row):
        copy.wait()
    total = row_sums[0]
    for r in range(1, rows):
        total = total + row_sums[r]
    out_ref[...] = total * factor


def pad_rows(array, count):
    return jnp.pad(array, (0, count * LANES - array.shape[0])).reshape(count, LANES)


def body(date_keys, product_keys, quantity, date_flags, category, unit_price, unit_cost):
    rows, grps = lax.axis_size("rows"), lax.axis_size("grp")
    facts = date_keys.shape[0]
    shard = unit_price.shape[0]
    flag_shard = date_flags.shape[0]
    flag_rows = cdiv(cdiv(flag_shard, LANES), 8) * 8
    table_rows = cdiv(cdiv(shard, LANES), 8) * 8
    fact_rows = cdiv(facts, 8 * LANES) * 8
    hi_cats = cdiv(CATS, LANES)
    size = 2 * hi_cats
    factor = CATS / (facts * rows * grps)

    flags = pad_rows(jnp.where(date_flags == 1, 1.0, 0.0), flag_rows)
    table = jnp.concatenate(
        [
            pad_rows(unit_price, table_rows),
            pad_rows(unit_price - unit_cost, table_rows),
            pad_rows(category.astype(jnp.float32), table_rows),
        ]
    )
    vmem = pl.BlockSpec(memory_space=pltpu.VMEM)
    ints = pltpu.VMEM((fact_rows, LANES), jnp.int32)
    cat_ints = pltpu.VMEM((rows * table_rows, LANES), jnp.int32)
    out = pl.pallas_call(
        functools.partial(kernel, rows, grps, flag_shard, shard, factor),
        out_shape=jax.ShapeDtypeStruct((size, LANES), jnp.float32),
        in_specs=[vmem] * 5,
        out_specs=vmem,
        scratch_shapes=[
            pltpu.VMEM((rows, flag_rows, LANES), jnp.float32),
            pltpu.VMEM((rows, 3 * table_rows, LANES), jnp.float32),
            ints,
            ints,
            ints,
            ints,
            ints,
            pltpu.VMEM((fact_rows, LANES), jnp.float32),
            pltpu.VMEM((SPLITS, fact_rows, LANES), jnp.float32),
            pltpu.VMEM((rows * table_rows, LANES), jnp.float32),
            pltpu.VMEM((2 * SPLITS, rows * table_rows, LANES), jnp.float32),
            cat_ints,
            cat_ints,
            pltpu.VMEM((grps, size, LANES), jnp.float32),
            pltpu.VMEM((rows, size, LANES), jnp.float32),
        ]
        + [pltpu.SemaphoreType.DMA((rows,))] * 4
        + [pltpu.SemaphoreType.DMA((grps,))] * 2
        + [pltpu.SemaphoreType.DMA((rows,))] * 2,
        compiler_params=pltpu.CompilerParams(collective_id=0, has_side_effects=True),
    )(
        flags,
        table,
        pad_rows(date_keys, fact_rows),
        pad_rows(product_keys, fact_rows),
        pad_rows(quantity, fact_rows),
    )
    return (
        out[:hi_cats].reshape(-1)[:CATS],
        out[hi_cats:].reshape(-1)[:CATS],
    )


def solution(mesh):
    return jax.shard_map(
        body,
        mesh=mesh,
        in_specs=(
            P(("rows", "grp")),
            P(("rows", "grp")),
            P(("rows", "grp")),
            P("rows"),
            P("rows"),
            P("rows"),
            P("rows"),
        ),
        out_specs=(P(), P()),
        check_vma=False,
    )
```

```python
import functools
import math

import jax
import jax.numpy as jnp
from jax import lax
from jax.experimental import pallas as pl
from jax.experimental.pallas import tpu as pltpu
from jax.sharding import PartitionSpec as P

CATS = 1000
LANES = 128
MESH = pl.DeviceIdType.MESH
NT = (((1,), (1,)), ((), ()))
SPLITS = 3


def cdiv(a, b):
    return (a + b - 1) // b


def split_bf16(value):
    parts = []
    for _ in range(SPLITS):
        part = value.astype(jnp.bfloat16).astype(jnp.float32)
        parts.append(part)
        value = value - part
    return parts


def divmod_const(keys, size, count):
    block = jnp.zeros_like(keys)
    for step in range(1, count):
        block = block + jnp.where(keys >= step * size, 1, 0)
    return block, keys - block * size


def packed_row(ref, *index):
    return jnp.broadcast_to(ref[index], (16, LANES)).astype(jnp.bfloat16)


def spots(count):
    shape = (count // 16, 16, LANES)
    tile = lax.broadcasted_iota(jnp.int32, shape, 0)
    line = lax.broadcasted_iota(jnp.int32, shape, 1)
    return (tile * 16 + line).astype(jnp.float32).astype(jnp.bfloat16)


def onehot(numbers, wanted):
    one = jnp.ones_like(numbers)
    hit = jnp.where(numbers == wanted[None], one, jnp.zeros_like(one))
    return hit.reshape(-1, LANES)


def to_dense(target, first, source, length):
    for i in range(cdiv(length, LANES)):
        width = min(LANES, length - i * LANES)
        target[pl.ds(first + i, 1), 0:width] = source(i * LANES, width)


def kernel(
    rows,
    grps,
    factor,
    flag_in,
    category_in,
    price_in,
    cost_in,
    date_in,
    product_in,
    quantity_in,
    out_ref,
    flags,
    flag_rows,
    raw_category,
    raw_price,
    raw_cost,
    tables,
    dates,
    products,
    quantity,
    date_row,
    date_word,
    date_bit,
    key_hi,
    key_lo,
    date_hot,
    hi_hot,
    lo_hot,
    word,
    kept,
    hist,
    values,
    cat_hi,
    cat_lo,
    grp_sums,
    row_sums,
    local,
    send_flag,
    recv_flag,
    send_table,
    recv_table,
    send_grp,
    recv_grp,
    send_row,
    recv_row,
):
    me = lax.axis_index("rows")
    mine = lax.axis_index("grp")
    flag_shard = flag_in.shape[1]
    shard = price_in.shape[1]
    table_rows = tables.shape[1] // 3
    fact_rows = dates.shape[0]
    all_rows = rows * table_rows
    hi_cats = cdiv(CATS, LANES)

    barrier = pltpu.get_barrier_semaphore()
    for step in range(1, rows):
        pl.semaphore_signal(
            barrier, inc=1, device_id=(lax.rem(me + step, rows), mine), device_id_type=MESH
        )
    for step in range(1, grps):
        pl.semaphore_signal(
            barrier, inc=1, device_id=(me, lax.rem(mine + step, grps)), device_id_type=MESH
        )
    inputs = [
        pltpu.make_async_copy(source, target, local.at[i])
        for i, (source, target) in enumerate(
            (
                (flag_in, flags.at[me]),
                (category_in, raw_category),
                (price_in, raw_price),
                (cost_in, raw_cost),
                (product_in, products),
                (date_in, dates),
                (quantity_in, quantity),
            )
        )
    ]
    for copy in inputs:
        copy.start()

    def to_rows(source, target, send, recv):
        copies = []
        for step in range(1, rows):
            copy = pltpu.make_async_remote_copy(
                src_ref=source,
                dst_ref=target,
                send_sem=send.at[step],
                recv_sem=recv.at[step],
                device_id=(lax.rem(me + step, rows), mine),
                device_id_type=MESH,
            )
            copy.start()
            copies.append(copy)
        return copies

    for copy in inputs[:4]:
        copy.wait()
    own = tables.at[me]
    last = cdiv(shard, LANES) - 1
    for i in range(3):
        own[pl.ds(i * table_rows + last, table_rows - last), :] = jnp.zeros(
            (table_rows - last, LANES), jnp.float32
        )
    to_dense(own, 0, lambda at, n: raw_price[:, at : at + n], shard)
    to_dense(
        own, table_rows, lambda at, n: raw_price[:, at : at + n] - raw_cost[:, at : at + n], shard
    )
    to_dense(
        own,
        2 * table_rows,
        lambda at, n: raw_category[:, at : at + n].astype(jnp.float32),
        shard,
    )
    pl.semaphore_wait(barrier, rows + grps - 2)
    flag_copies = to_rows(flags.at[me], flags.at[me], send_flag, recv_flag)
    table_copies = to_rows(tables.at[me], tables.at[me], send_table, recv_table)

    for copy in inputs[4:]:
        copy.wait()
    block, inside = divmod_const(dates[...], flag_shard, rows)
    date_row[...] = (
        block * cdiv(flag_shard, LANES) + jnp.right_shift(inside, 7)
    ).astype(jnp.float32)
    date_word[...] = (jnp.right_shift(inside, 3) & 15).astype(jnp.float32)
    date_bit[...] = inside & 7
    block, inside = divmod_const(products[...], shard, rows)
    key_hi[...] = (block * table_rows + jnp.right_shift(inside, 7)).astype(jnp.float32)
    key_lo[...] = (inside & (LANES - 1)).astype(jnp.float32)
    flag_rows[...] = jnp.zeros_like(flag_rows)
    hist[...] = jnp.zeros_like(hist)
    all_flag_rows = flag_rows.shape[0]

    @pl.loop(0, fact_rows // 8)
    def _(chunk):
        base = chunk * 8
        numbers = spots(LANES)
        for i in range(8):
            line = (pl.ds(base + i, 1), slice(None))
            here = slice(i * LANES, (i + 1) * LANES)
            lo_hot[chunk, :, here] = onehot(numbers, packed_row(key_lo, *line))
            for first in range(0, all_rows, LANES):
                wanted = key_hi[line] - float(first)
                wanted = jnp.broadcast_to(wanted, (16, LANES)).astype(jnp.bfloat16)
                hi_hot[chunk, first : first + LANES, here] = onehot(numbers, wanted)
            for first in range(0, all_flag_rows, LANES):
                count = min(LANES, all_flag_rows - first)
                wanted = date_row[line] - float(first)
                wanted = jnp.broadcast_to(wanted, (16, LANES)).astype(jnp.bfloat16)
                date_hot[chunk, first : first + count, here] = onehot(spots(count), wanted)

    lane = lax.broadcasted_iota(jnp.int32, (16, LANES), 1)
    place = lax.broadcasted_iota(jnp.int32, (16, LANES), 0)
    weight = jnp.where(
        jnp.right_shift(lane, 3) == place, jnp.left_shift(jnp.ones_like(lane), lane & 7), 0
    ).astype(jnp.float32).astype(jnp.bfloat16)
    place = place.astype(jnp.float32)

    for copy in flag_copies:
        copy.wait()
    for r in range(rows):
        to_dense(
            flag_rows,
            r * cdiv(flag_shard, LANES),
            lambda at, n: jnp.where(flags[r, :, at : at + n] == 1, 1.0, 0.0),
            flag_shard,
        )
    words = lax.dot_general(
        weight, flag_rows[...].astype(jnp.bfloat16), NT, preferred_element_type=jnp.float32
    ).astype(jnp.bfloat16)

    @pl.loop(0, fact_rows // 8)
    def _(chunk):
        base = chunk * 8
        found = jnp.dot(words, date_hot[chunk], preferred_element_type=jnp.float32)
        for i in range(8):
            piece = found[:, i * LANES : (i + 1) * LANES]
            picked = jnp.where(place == date_word[pl.ds(base + i, 1), :], piece, 0.0)
            word[pl.ds(base + i, 1), :] = jnp.sum(picked, axis=0, keepdims=True)

    passed = jnp.right_shift(word[...].astype(jnp.int32), date_bit[...]) & 1
    for s, part in enumerate(split_bf16(jnp.where(passed == 1, quantity[...], 0.0))):
        kept[s] = part

    @pl.loop(0, fact_rows // 8)
    def _(chunk):
        base = chunk * 8
        right = lo_hot[chunk]
        amounts = []
        for s in range(SPLITS):
            lines = [packed_row(kept, s, pl.ds(base + i, 1), slice(None)) for i in range(8)]
            amount = jnp.concatenate(lines, axis=1)
            scaled = right.reshape(LANES // 16, 16, 8 * LANES) * amount[None]
            amounts.append(scaled.reshape(LANES, 8 * LANES))
        for first in range(0, all_rows, LANES):
            left = hi_hot[chunk, first : first + LANES, :]
            total = hist[pl.ds(first, LANES), :]
            for s in range(SPLITS):
                total = total + lax.dot_general(
                    left, amounts[s], NT, preferred_element_type=jnp.float32
                )
            hist[pl.ds(first, LANES), :] = total

    for copy in table_copies:
        copy.wait()

    @pl.loop(0, rows)
    def _(r):
        spot = pl.ds(pl.multiple_of(r * table_rows, table_rows), table_rows)
        amount = hist[spot, :]
        table = tables[r]
        category = table[2 * table_rows :].astype(jnp.int32)
        cat_hi[spot, :] = jnp.right_shift(category, 7).astype(jnp.float32)
        cat_lo[spot, :] = (category & (LANES - 1)).astype(jnp.float32)
        for s, part in enumerate(split_bf16(amount * table[:table_rows])):
            values[2 * s, spot, :] = part
        for s, part in enumerate(split_bf16(amount * table[table_rows : 2 * table_rows])):
            values[2 * s + 1, spot, :] = part

    cat_iota = lax.broadcasted_iota(jnp.int32, (hi_cats, LANES), 0).astype(jnp.float32)

    def add_products(chunk, running):
        base = chunk * 8
        numbers = spots(LANES)
        lefts, rights = [], []
        for i in range(8):
            line = (pl.ds(base + i, 1), slice(None))
            mask = cat_iota == cat_hi[line]
            lefts.append(
                jnp.concatenate(
                    [jnp.where(mask, values[v, line[0], :], 0.0) for v in range(2 * SPLITS)],
                    axis=0,
                ).astype(jnp.bfloat16)
            )
            rights.append(onehot(numbers, packed_row(cat_lo, *line)))
        return running + lax.dot_general(
            jnp.concatenate(lefts, axis=1),
            jnp.concatenate(rights, axis=1),
            NT,
            preferred_element_type=jnp.float32,
        )

    summed = lax.fori_loop(
        0,
        all_rows // 8,
        add_products,
        jnp.zeros((2 * SPLITS * hi_cats, LANES), jnp.float32),
    )
    size = 2 * hi_cats
    partial = summed[:size]
    for s in range(1, SPLITS):
        partial = partial + summed[s * size : (s + 1) * size]

    grp_sums[pl.ds(mine, 1)] = partial[None]
    copies = []
    for step in range(1, grps):
        copy = pltpu.make_async_remote_copy(
            src_ref=grp_sums.at[mine],
            dst_ref=grp_sums.at[mine],
            send_sem=send_grp.at[step],
            recv_sem=recv_grp.at[step],
            device_id=(me, lax.rem(mine + step, grps)),
            device_id_type=MESH,
        )
        copy.start()
        copies.append(copy)
    for copy in copies:
        copy.wait_recv()
    total = grp_sums[0]
    for g in range(1, grps):
        total = total + grp_sums[g]

    row_sums[pl.ds(me, 1)] = total[None]
    last_copies = to_rows(row_sums.at[me], row_sums.at[me], send_row, recv_row)
    for copy in copies:
        copy.wait_send()
    for copy in last_copies:
        copy.wait()
    total = row_sums[0]
    for r in range(1, rows):
        total = total + row_sums[r]
    out_ref[...] = total * factor


def body(date_keys, product_keys, quantity, date_flags, category, unit_price, unit_cost):
    rows, grps = lax.axis_size("rows"), lax.axis_size("grp")
    facts = date_keys.shape[0]
    shard = unit_price.shape[0]
    flag_shard = date_flags.shape[0]
    table_rows = cdiv(cdiv(shard, LANES), 16) * 16
    fact_rows = cdiv(facts, 8 * LANES) * 8
    chunks = fact_rows // 8
    all_rows = cdiv(rows * table_rows, LANES) * LANES
    all_flag_rows = cdiv(rows * cdiv(flag_shard, LANES), 16) * 16
    hi_cats = cdiv(CATS, LANES)
    size = 2 * hi_cats
    factor = CATS / (facts * rows * grps)

    def by_rows(array):
        return jnp.pad(array, (0, fact_rows * LANES - facts)).reshape(fact_rows, LANES)

    f32, i32, bf16 = jnp.float32, jnp.int32, jnp.bfloat16
    dense = (fact_rows, LANES)
    scratch = [
        ((rows, 1, flag_shard), i32),
        ((all_flag_rows, LANES), f32),
        ((1, shard), i32),
        ((1, shard), f32),
        ((1, shard), f32),
        ((rows, 3 * table_rows, LANES), f32),
        (dense, i32),
        (dense, i32),
        (dense, f32),
        (dense, f32),
        (dense, f32),
        (dense, i32),
        (dense, f32),
        (dense, f32),
        ((chunks, all_flag_rows, 8 * LANES), bf16),
        ((chunks, all_rows, 8 * LANES), bf16),
        ((chunks, LANES, 8 * LANES), bf16),
        (dense, f32),
        ((SPLITS,) + dense, f32),
        ((all_rows, LANES), f32),
        ((2 * SPLITS, all_rows, LANES), f32),
        ((all_rows, LANES), f32),
        ((all_rows, LANES), f32),
        ((grps, size, LANES), f32),
        ((rows, size, LANES), f32),
    ]
    bytes_held = sum(math.prod(shape) * jnp.dtype(kind).itemsize for shape, kind in scratch)
    out = pl.pallas_call(
        functools.partial(kernel, rows, grps, factor),
        out_shape=jax.ShapeDtypeStruct((size, LANES), f32),
        in_specs=[pl.BlockSpec(memory_space=pl.ANY)] * 7,
        out_specs=pl.BlockSpec(memory_space=pltpu.VMEM),
        scratch_shapes=[pltpu.VMEM(shape, kind) for shape, kind in scratch]
        + [pltpu.SemaphoreType.DMA((7,))]
        + [pltpu.SemaphoreType.DMA((rows,))] * 4
        + [pltpu.SemaphoreType.DMA((grps,))] * 2
        + [pltpu.SemaphoreType.DMA((rows,))] * 2,
        compiler_params=pltpu.CompilerParams(
            collective_id=0,
            has_side_effects=True,
            vmem_limit_bytes=2 * bytes_held + (8 << 20),
        ),
    )(
        date_flags.reshape(1, -1),
        category.reshape(1, -1),
        unit_price.reshape(1, -1),
        unit_cost.reshape(1, -1),
        by_rows(date_keys),
        by_rows(product_keys),
        by_rows(quantity),
    )
    return (
        out[:hi_cats].reshape(-1)[:CATS],
        out[hi_cats:].reshape(-1)[:CATS],
    )


def solution(mesh):
    return jax.shard_map(
        body,
        mesh=mesh,
        in_specs=(
            P(("rows", "grp")),
            P(("rows", "grp")),
            P(("rows", "grp")),
            P("rows"),
            P("rows"),
            P("rows"),
            P("rows"),
        ),
        out_specs=(P(), P()),
        check_vma=False,
    )
```

```python
import functools

import jax
import jax.numpy as jnp
from jax import lax
from jax.experimental import pallas as pl
from jax.experimental.pallas import tpu as pltpu
from jax.sharding import PartitionSpec as P

CATS = 1000
LANES = 128
MESH = pl.DeviceIdType.MESH
NT = (((1,), (1,)), ((), ()))
SPLITS = 3


def cdiv(a, b):
    return (a + b - 1) // b


def split_bf16(value):
    parts = []
    for _ in range(SPLITS):
        part = value.astype(jnp.bfloat16).astype(jnp.float32)
        parts.append(part)
        value = value - part
    return parts


def divmod_const(keys, size, count):
    block = jnp.zeros_like(keys)
    for step in range(1, count):
        block = block + jnp.where(keys >= step * size, 1, 0)
    return block, keys - block * size


def packed_row(ref, *index):
    return jnp.broadcast_to(ref[index], (16, LANES)).astype(jnp.bfloat16)


def spots(count):
    shape = (count // 16, 16, LANES)
    tile = lax.broadcasted_iota(jnp.int32, shape, 0)
    line = lax.broadcasted_iota(jnp.int32, shape, 1)
    return (tile * 16 + line).astype(jnp.float32).astype(jnp.bfloat16)


def onehot(numbers, wanted):
    one = jnp.ones_like(numbers)
    hit = jnp.where(numbers == wanted[None], one, jnp.zeros_like(one))
    return hit.reshape(-1, LANES)


def to_dense(target, first, source, length):
    for i in range(cdiv(length, LANES)):
        width = min(LANES, length - i * LANES)
        target[pl.ds(first + i, 1), 0:width] = source(i * LANES, width)


def kernel(
    rows,
    grps,
    factor,
    flag_in,
    category_in,
    price_in,
    cost_in,
    date_in,
    product_in,
    quantity_in,
    out_ref,
    flags,
    flag_rows,
    raw_category,
    raw_price,
    raw_cost,
    tables,
    dates,
    products,
    quantity,
    date_row,
    date_word,
    date_bit,
    key_hi,
    key_lo,
    date_hot,
    hi_hot,
    lo_hot,
    word,
    kept,
    hist,
    values,
    cat_hi,
    cat_lo,
    grp_sums,
    row_sums,
    local,
    send_flag,
    recv_flag,
    send_table,
    recv_table,
    send_grp,
    recv_grp,
    send_row,
    recv_row,
):
    me = lax.axis_index("rows")
    mine = lax.axis_index("grp")
    flag_shard = flag_in.shape[0]
    shard = price_in.shape[1]
    table_rows = tables.shape[1] // 3
    fact_rows = dates.shape[0]
    all_rows = rows * table_rows
    hi_cats = cdiv(CATS, LANES)

    barrier = pltpu.get_barrier_semaphore()
    for step in range(1, rows):
        pl.semaphore_signal(
            barrier, inc=1, device_id=(lax.rem(me + step, rows), mine), device_id_type=MESH
        )
    for step in range(1, grps):
        pl.semaphore_signal(
            barrier, inc=1, device_id=(me, lax.rem(mine + step, grps)), device_id_type=MESH
        )
    inputs = [
        pltpu.make_async_copy(source, target, local.at[i])
        for i, (source, target) in enumerate(
            (
                (flag_in, flags.at[me, 0]),
                (category_in, raw_category),
                (price_in, raw_price),
                (cost_in, raw_cost),
                (product_in, products),
                (date_in, dates),
                (quantity_in, quantity),
            )
        )
    ]
    for copy in inputs:
        copy.start()

    def to_rows(source, target, send, recv):
        copies = []
        for step in range(1, rows):
            copy = pltpu.make_async_remote_copy(
                src_ref=source,
                dst_ref=target,
                send_sem=send.at[step],
                recv_sem=recv.at[step],
                device_id=(lax.rem(me + step, rows), mine),
                device_id_type=MESH,
            )
            copy.start()
            copies.append(copy)
        return copies

    for copy in inputs[:4]:
        copy.wait()
    own = tables.at[me]
    last = cdiv(shard, LANES) - 1
    for i in range(3):
        own[pl.ds(i * table_rows + last, table_rows - last), :] = jnp.zeros(
            (table_rows - last, LANES), jnp.float32
        )
    to_dense(own, 0, lambda at, n: raw_price[:, at : at + n], shard)
    to_dense(
        own, table_rows, lambda at, n: raw_price[:, at : at + n] - raw_cost[:, at : at + n], shard
    )
    to_dense(
        own,
        2 * table_rows,
        lambda at, n: raw_category[:, at : at + n].astype(jnp.float32),
        shard,
    )
    pl.semaphore_wait(barrier, rows + grps - 2)
    flag_copies = to_rows(flags.at[me], flags.at[me], send_flag, recv_flag)
    table_copies = to_rows(tables.at[me], tables.at[me], send_table, recv_table)

    for copy in inputs[4:]:
        copy.wait()
    block, inside = divmod_const(dates[...], flag_shard, rows)
    date_row[...] = (
        block * cdiv(flag_shard, LANES) + jnp.right_shift(inside, 7)
    ).astype(jnp.float32)
    date_word[...] = (jnp.right_shift(inside, 3) & 15).astype(jnp.float32)
    date_bit[...] = inside & 7
    block, inside = divmod_const(products[...], shard, rows)
    key_hi[...] = (block * table_rows + jnp.right_shift(inside, 7)).astype(jnp.float32)
    key_lo[...] = (inside & (LANES - 1)).astype(jnp.float32)
    flag_rows[...] = jnp.zeros_like(flag_rows)
    hist[...] = jnp.zeros_like(hist)
    all_flag_rows = flag_rows.shape[0]

    @pl.loop(0, fact_rows // 8)
    def _(chunk):
        base = chunk * 8
        numbers = spots(LANES)
        for i in range(8):
            line = (pl.ds(base + i, 1), slice(None))
            here = slice(i * LANES, (i + 1) * LANES)
            lo_hot[chunk, :, here] = onehot(numbers, packed_row(key_lo, *line))
            for first in range(0, all_rows, LANES):
                wanted = key_hi[line] - float(first)
                wanted = jnp.broadcast_to(wanted, (16, LANES)).astype(jnp.bfloat16)
                hi_hot[chunk, first : first + LANES, here] = onehot(numbers, wanted)
            for first in range(0, all_flag_rows, LANES):
                count = min(LANES, all_flag_rows - first)
                wanted = date_row[line] - float(first)
                wanted = jnp.broadcast_to(wanted, (16, LANES)).astype(jnp.bfloat16)
                date_hot[chunk, first : first + count, here] = onehot(spots(count), wanted)

    lane = lax.broadcasted_iota(jnp.int32, (16, LANES), 1)
    place = lax.broadcasted_iota(jnp.int32, (16, LANES), 0)
    weight = jnp.where(
        jnp.right_shift(lane, 3) == place, jnp.left_shift(jnp.ones_like(lane), lane & 7), 0
    ).astype(jnp.float32).astype(jnp.bfloat16)
    place = place.astype(jnp.float32)

    for copy in flag_copies:
        copy.wait()
    for r in range(rows):
        to_dense(
            flag_rows,
            r * cdiv(flag_shard, LANES),
            lambda at, n: jnp.where(flags[r, :, at : at + n] == 1, 1.0, 0.0),
            flag_shard,
        )
    words = lax.dot_general(
        weight, flag_rows[...].astype(jnp.bfloat16), NT, preferred_element_type=jnp.float32
    ).astype(jnp.bfloat16)

    @pl.loop(0, fact_rows // 8)
    def _(chunk):
        base = chunk * 8
        found = jnp.dot(words, date_hot[chunk], preferred_element_type=jnp.float32)
        for i in range(8):
            piece = found[:, i * LANES : (i + 1) * LANES]
            picked = jnp.where(place == date_word[pl.ds(base + i, 1), :], piece, 0.0)
            word[pl.ds(base + i, 1), :] = jnp.sum(picked, axis=0, keepdims=True)

    passed = jnp.right_shift(word[...].astype(jnp.int32), date_bit[...]) & 1
    for s, part in enumerate(split_bf16(jnp.where(passed == 1, quantity[...], 0.0))):
        kept[s] = part

    @pl.loop(0, fact_rows // 8)
    def _(chunk):
        base = chunk * 8
        right = lo_hot[chunk]
        amounts = []
        for s in range(SPLITS):
            lines = [packed_row(kept, s, pl.ds(base + i, 1), slice(None)) for i in range(8)]
            amount = jnp.concatenate(lines, axis=1)
            scaled = right.reshape(LANES // 16, 16, 8 * LANES) * amount[None]
            amounts.append(scaled.reshape(LANES, 8 * LANES))
        for first in range(0, all_rows, LANES):
            left = hi_hot[chunk, first : first + LANES, :]
            total = hist[pl.ds(first, LANES), :]
            for s in range(SPLITS):
                total = total + lax.dot_general(
                    left, amounts[s], NT, preferred_element_type=jnp.float32
                )
            hist[pl.ds(first, LANES), :] = total

    for copy in table_copies:
        copy.wait()

    @pl.loop(0, rows)
    def _(r):
        spot = pl.ds(pl.multiple_of(r * table_rows, table_rows), table_rows)
        amount = hist[spot, :]
        table = tables[r]
        category = table[2 * table_rows :].astype(jnp.int32)
        cat_hi[spot, :] = jnp.right_shift(category, 7).astype(jnp.float32)
        cat_lo[spot, :] = (category & (LANES - 1)).astype(jnp.float32)
        for s, part in enumerate(split_bf16(amount * table[:table_rows])):
            values[2 * s, spot, :] = part
        for s, part in enumerate(split_bf16(amount * table[table_rows : 2 * table_rows])):
            values[2 * s + 1, spot, :] = part

    cat_iota = lax.broadcasted_iota(jnp.int32, (hi_cats, LANES), 0).astype(jnp.float32)

    def add_products(chunk, running):
        base = chunk * 8
        numbers = spots(LANES)
        lefts, rights = [], []
        for i in range(8):
            line = (pl.ds(base + i, 1), slice(None))
            mask = cat_iota == cat_hi[line]
            lefts.append(
                jnp.concatenate(
                    [jnp.where(mask, values[v, line[0], :], 0.0) for v in range(2 * SPLITS)],
                    axis=0,
                ).astype(jnp.bfloat16)
            )
            rights.append(onehot(numbers, packed_row(cat_lo, *line)))
        return running + lax.dot_general(
            jnp.concatenate(lefts, axis=1),
            jnp.concatenate(rights, axis=1),
            NT,
            preferred_element_type=jnp.float32,
        )

    summed = lax.fori_loop(
        0,
        all_rows // 8,
        add_products,
        jnp.zeros((2 * SPLITS * hi_cats, LANES), jnp.float32),
    )
    size = 2 * hi_cats
    partial = summed[:size]
    for s in range(1, SPLITS):
        partial = partial + summed[s * size : (s + 1) * size]

    grp_sums[pl.ds(mine, 1)] = partial[None]
    copies = []
    for step in range(1, grps):
        copy = pltpu.make_async_remote_copy(
            src_ref=grp_sums.at[mine],
            dst_ref=grp_sums.at[mine],
            send_sem=send_grp.at[step],
            recv_sem=recv_grp.at[step],
            device_id=(me, lax.rem(mine + step, grps)),
            device_id_type=MESH,
        )
        copy.start()
        copies.append(copy)
    for copy in copies:
        copy.wait_recv()
    total = grp_sums[0]
    for g in range(1, grps):
        total = total + grp_sums[g]

    row_sums[pl.ds(me, 1)] = total[None]
    last_copies = to_rows(row_sums.at[me], row_sums.at[me], send_row, recv_row)
    for copy in copies:
        copy.wait_send()
    for copy in last_copies:
        copy.wait()
    total = row_sums[0]
    for r in range(1, rows):
        total = total + row_sums[r]
    out_ref[...] = total * factor


def body(date_keys, product_keys, quantity, date_flags, category, unit_price, unit_cost):
    rows, grps = lax.axis_size("rows"), lax.axis_size("grp")
    facts = date_keys.shape[0]
    shard = unit_price.shape[0]
    flag_shard = date_flags.shape[0]
    table_rows = cdiv(cdiv(shard, LANES), 16) * 16
    fact_rows = cdiv(facts, 8 * LANES) * 8
    chunks = fact_rows // 8
    all_rows = cdiv(rows * table_rows, LANES) * LANES
    all_flag_rows = cdiv(rows * cdiv(flag_shard, LANES), 16) * 16
    hi_cats = cdiv(CATS, LANES)
    size = 2 * hi_cats
    factor = CATS / (facts * rows * grps)

    def by_rows(array):
        return jnp.pad(array, (0, fact_rows * LANES - facts)).reshape(fact_rows, LANES)

    f32, i32, bf16 = jnp.float32, jnp.int32, jnp.bfloat16
    dense = (fact_rows, LANES)
    scratch = [
        ((rows, 1, flag_shard), i32),
        ((all_flag_rows, LANES), f32),
        ((1, shard), i32),
        ((1, shard), f32),
        ((1, shard), f32),
        ((rows, 3 * table_rows, LANES), f32),
        (dense, i32),
        (dense, i32),
        (dense, f32),
        (dense, f32),
        (dense, f32),
        (dense, i32),
        (dense, f32),
        (dense, f32),
        ((chunks, all_flag_rows, 8 * LANES), bf16),
        ((chunks, all_rows, 8 * LANES), bf16),
        ((chunks, LANES, 8 * LANES), bf16),
        (dense, f32),
        ((SPLITS,) + dense, f32),
        ((all_rows, LANES), f32),
        ((2 * SPLITS, all_rows, LANES), f32),
        ((all_rows, LANES), f32),
        ((all_rows, LANES), f32),
        ((grps, size, LANES), f32),
        ((rows, size, LANES), f32),
    ]
    out = pl.pallas_call(
        functools.partial(kernel, rows, grps, factor),
        out_shape=jax.ShapeDtypeStruct((size, LANES), f32),
        in_specs=[pl.BlockSpec(memory_space=pltpu.HBM)] * 7,
        out_specs=pl.BlockSpec(memory_space=pltpu.VMEM),
        scratch_shapes=[pltpu.VMEM(shape, kind) for shape, kind in scratch]
        + [pltpu.SemaphoreType.DMA((7,))]
        + [pltpu.SemaphoreType.DMA((rows,))] * 4
        + [pltpu.SemaphoreType.DMA((grps,))] * 2
        + [pltpu.SemaphoreType.DMA((rows,))] * 2,
        compiler_params=pltpu.CompilerParams(
            collective_id=0,
            has_side_effects=True,
        ),
    )(
        date_flags,
        category.reshape(1, -1),
        unit_price.reshape(1, -1),
        unit_cost.reshape(1, -1),
        by_rows(date_keys),
        by_rows(product_keys),
        by_rows(quantity),
    )
    return (
        out[:hi_cats].reshape(-1)[:CATS],
        out[hi_cats:].reshape(-1)[:CATS],
    )


def solution(mesh):
    return jax.shard_map(
        body,
        mesh=mesh,
        in_specs=(
            P(("rows", "grp")),
            P(("rows", "grp")),
            P(("rows", "grp")),
            P("rows"),
            P("rows"),
            P("rows"),
            P("rows"),
        ),
        out_specs=(P(), P()),
        check_vma=False,
    )
```

```python
import functools

import jax
import jax.numpy as jnp
from jax import lax
from jax.experimental import pallas as pl
from jax.experimental.pallas import tpu as pltpu
from jax.sharding import PartitionSpec as P

CATS = 1000
LANES = 128
MESH = pl.DeviceIdType.MESH
NT = (((1,), (1,)), ((), ()))
SPLITS = 3
STEP = 32
FACT_STEP = 32


def cdiv(a, b):
    return (a + b - 1) // b


def split_bf16(value):
    parts = []
    for _ in range(SPLITS):
        part = value.astype(jnp.bfloat16).astype(jnp.float32)
        parts.append(part)
        value = value - part
    return parts


def divmod_const(keys, size, count):
    block = jnp.zeros_like(keys)
    for step in range(1, count):
        block = block + jnp.where(keys >= step * size, 1, 0)
    return block, keys - block * size


def packed_row(ref, *index):
    return jnp.broadcast_to(ref[index], (16, LANES)).astype(jnp.bfloat16)


def spots(count):
    line = lax.broadcasted_iota(jnp.int32, (16, LANES), 0).astype(jnp.float32)
    return [(line + float(first)).astype(jnp.bfloat16) for first in range(0, count, 16)]


def marked(numbers, wanted, amount):
    zero = jnp.zeros_like(wanted)
    return jnp.concatenate(
        [jnp.where(tile == wanted, amount, zero) for tile in numbers], axis=0
    )


def to_dense(target, first, source, length):
    for i in range(cdiv(length, LANES)):
        width = min(LANES, length - i * LANES)
        target[pl.ds(first + i, 1), 0:width] = source(i * LANES, width)


def kernel(
    rows,
    grps,
    factor,
    flag_in,
    category_in,
    price_in,
    cost_in,
    date_in,
    product_in,
    quantity_in,
    out_ref,
    flags,
    flag_rows,
    raw_category,
    raw_price,
    raw_cost,
    tables,
    dates,
    products,
    quantity,
    date_row,
    date_word,
    date_bit,
    key_hi,
    key_lo,
    word,
    kept,
    hist,
    values,
    cat_hi,
    cat_lo,
    grp_sums,
    row_sums,
    local,
    send_flag,
    recv_flag,
    send_table,
    recv_table,
    send_grp,
    recv_grp,
    send_row,
    recv_row,
):
    me = lax.axis_index("rows")
    mine = lax.axis_index("grp")
    flag_shard = flag_in.shape[0]
    shard = price_in.shape[1]
    table_rows = tables.shape[1] // 3
    fact_rows = dates.shape[0]
    all_rows = rows * table_rows
    hi_cats = cdiv(CATS, LANES)

    barrier = pltpu.get_barrier_semaphore()
    for step in range(1, rows):
        pl.semaphore_signal(
            barrier, inc=1, device_id=(lax.rem(me + step, rows), mine), device_id_type=MESH
        )
    for step in range(1, grps):
        pl.semaphore_signal(
            barrier, inc=1, device_id=(me, lax.rem(mine + step, grps)), device_id_type=MESH
        )
    inputs = [
        pltpu.make_async_copy(source, target, local.at[i])
        for i, (source, target) in enumerate(
            (
                (flag_in, flags.at[me, 0]),
                (category_in, raw_category),
                (price_in, raw_price),
                (cost_in, raw_cost),
                (product_in, products),
                (date_in, dates),
                (quantity_in, quantity),
            )
        )
    ]
    for copy in inputs:
        copy.start()

    def to_rows(source, target, send, recv):
        copies = []
        for step in range(1, rows):
            copy = pltpu.make_async_remote_copy(
                src_ref=source,
                dst_ref=target,
                send_sem=send.at[step],
                recv_sem=recv.at[step],
                device_id=(lax.rem(me + step, rows), mine),
                device_id_type=MESH,
            )
            copy.start()
            copies.append(copy)
        return copies

    for copy in inputs[:4]:
        copy.wait()
    own = tables.at[me]
    last = cdiv(shard, LANES) - 1
    for i in range(3):
        own[pl.ds(i * table_rows + last, table_rows - last), :] = jnp.zeros(
            (table_rows - last, LANES), jnp.float32
        )
    to_dense(own, 0, lambda at, n: raw_price[:, at : at + n], shard)
    to_dense(
        own, table_rows, lambda at, n: raw_price[:, at : at + n] - raw_cost[:, at : at + n], shard
    )
    to_dense(
        own,
        2 * table_rows,
        lambda at, n: raw_category[:, at : at + n].astype(jnp.float32),
        shard,
    )
    pl.semaphore_wait(barrier, rows + grps - 2)
    flag_copies = to_rows(flags.at[me], flags.at[me], send_flag, recv_flag)
    table_copies = to_rows(tables.at[me], tables.at[me], send_table, recv_table)

    for copy in inputs[4:]:
        copy.wait()
    block, inside = divmod_const(dates[...], flag_shard, rows)
    date_row[...] = (
        block * cdiv(flag_shard, LANES) + jnp.right_shift(inside, 7)
    ).astype(jnp.float32)
    date_word[...] = (jnp.right_shift(inside, 3) & 15).astype(jnp.float32)
    date_bit[...] = inside & 7
    block, inside = divmod_const(products[...], shard, rows)
    line = block * table_rows + jnp.right_shift(inside, 7)
    half = jnp.right_shift(line, 6) & 1
    key_hi[...] = (jnp.right_shift(line, 7) * 64 + (line & 63)).astype(jnp.float32)
    key_lo[...] = ((inside & (LANES - 1)) + half * LANES).astype(jnp.float32)
    flag_rows[...] = jnp.zeros_like(flag_rows)
    hist[...] = jnp.zeros_like(hist)
    all_flag_rows = flag_rows.shape[0]

    lane = lax.broadcasted_iota(jnp.int32, (16, LANES), 1)
    place = lax.broadcasted_iota(jnp.int32, (16, LANES), 0)
    weight = jnp.where(
        jnp.right_shift(lane, 3) == place, jnp.left_shift(jnp.ones_like(lane), lane & 7), 0
    ).astype(jnp.float32).astype(jnp.bfloat16)
    place = place.astype(jnp.float32)

    for copy in flag_copies:
        copy.wait()
    for r in range(rows):
        to_dense(
            flag_rows,
            r * cdiv(flag_shard, LANES),
            lambda at, n: jnp.where(flags[r, :, at : at + n] == 1, 1.0, 0.0),
            flag_shard,
        )
    words = lax.dot_general(
        weight, flag_rows[...].astype(jnp.bfloat16), NT, preferred_element_type=jnp.float32
    ).astype(jnp.bfloat16)

    @pl.loop(0, fact_rows // FACT_STEP)
    def _(chunk):
        base = chunk * FACT_STEP
        numbers = spots(all_flag_rows)
        lines = [packed_row(date_row, pl.ds(base + i, 1), slice(None)) for i in range(FACT_STEP)]
        hot = jnp.concatenate(
            [marked(numbers, line, jnp.ones_like(line)) for line in lines], axis=1
        )
        found = jnp.dot(words, hot, preferred_element_type=jnp.float32)
        for i in range(FACT_STEP):
            piece = found[:, i * LANES : (i + 1) * LANES]
            picked = jnp.where(place == date_word[pl.ds(base + i, 1), :], piece, 0.0)
            word[pl.ds(base + i, 1), :] = jnp.sum(picked, axis=0, keepdims=True)

    passed = jnp.right_shift(word[...].astype(jnp.int32), date_bit[...]) & 1
    for s, part in enumerate(split_bf16(jnp.where(passed == 1, quantity[...], 0.0))):
        kept[s] = part

    @pl.loop(0, fact_rows // FACT_STEP)
    def _(chunk):
        base = chunk * FACT_STEP
        numbers, row_numbers = spots(2 * LANES), spots(64)
        lows = [packed_row(key_lo, pl.ds(base + i, 1), slice(None)) for i in range(FACT_STEP)]
        right = jnp.concatenate([marked(numbers, low, jnp.ones_like(low)) for low in lows], axis=1)
        amounts = [
            [packed_row(kept, s, pl.ds(base + i, 1), slice(None)) for s in range(SPLITS)]
            for i in range(FACT_STEP)
        ]
        for first in range(0, all_rows, LANES):
            lefts = []
            for i in range(FACT_STEP):
                wanted = jnp.broadcast_to(key_hi[pl.ds(base + i, 1), :] - float(first // 2), (16, LANES))
                wanted = wanted.astype(jnp.bfloat16)
                lefts.append(
                    jnp.concatenate(
                        [marked(row_numbers, wanted, amount) for amount in amounts[i]], axis=0
                    )
                )
            summed = lax.dot_general(
                jnp.concatenate(lefts, axis=1), right, NT, preferred_element_type=jnp.float32
            )
            total = summed[:64]
            for s in range(1, SPLITS):
                total = total + summed[s * 64 : (s + 1) * 64]
            hist[pl.ds(first, 64), :] += total[:, :LANES]
            hist[pl.ds(first + 64, 64), :] += total[:, LANES:]

    for copy in table_copies:
        copy.wait()

    @pl.loop(0, rows)
    def _(r):
        spot = pl.ds(pl.multiple_of(r * table_rows, table_rows), table_rows)
        amount = hist[spot, :]
        table = tables[r]
        category = table[2 * table_rows :].astype(jnp.int32)
        half = jnp.right_shift(category, 6) & 1
        cat_hi[spot, :] = (jnp.right_shift(category, 7) + half * hi_cats).astype(jnp.float32)
        cat_lo[spot, :] = (category & (LANES // 2 - 1)).astype(jnp.float32)
        for s, part in enumerate(split_bf16(amount * table[:table_rows])):
            values[2 * s, spot, :] = part
        for s, part in enumerate(split_bf16(amount * table[table_rows : 2 * table_rows])):
            values[2 * s + 1, spot, :] = part

    halves = cdiv(2 * hi_cats, 16) * 16

    def add_products(chunk, running):
        base = chunk * STEP
        row_numbers, numbers = spots(halves), spots(LANES // 2)
        lefts, rights = [], []
        for i in range(STEP):
            line = (pl.ds(base + i, 1), slice(None))
            wanted = packed_row(cat_hi, *line)
            lefts.append(
                jnp.concatenate(
                    [
                        marked(row_numbers, wanted, packed_row(values, v, *line))
                        for v in range(2 * SPLITS)
                    ],
                    axis=0,
                )
            )
            low = packed_row(cat_lo, *line)
            rights.append(marked(numbers, low, jnp.ones_like(low)))
        summed = lax.dot_general(
            jnp.concatenate(lefts, axis=1),
            jnp.concatenate(rights, axis=1),
            NT,
            preferred_element_type=jnp.float32,
        )
        for s in range(SPLITS):
            running = running + summed[2 * s * halves : 2 * (s + 1) * halves]
        return running

    summed = lax.fori_loop(
        0,
        all_rows // STEP,
        add_products,
        jnp.zeros((2 * halves, LANES // 2), jnp.float32),
    )
    outputs = []
    for v in range(2):
        whole = summed[v * halves : (v + 1) * halves]
        outputs.append(
            jnp.concatenate([whole[:hi_cats], whole[hi_cats : 2 * hi_cats]], axis=1)
        )
    partial = jnp.concatenate(outputs, axis=0)

    grp_sums[pl.ds(mine, 1)] = partial[None]
    copies = []
    for step in range(1, grps):
        copy = pltpu.make_async_remote_copy(
            src_ref=grp_sums.at[mine],
            dst_ref=grp_sums.at[mine],
            send_sem=send_grp.at[step],
            recv_sem=recv_grp.at[step],
            device_id=(me, lax.rem(mine + step, grps)),
            device_id_type=MESH,
        )
        copy.start()
        copies.append(copy)
    for copy in copies:
        copy.wait_recv()
    total = grp_sums[0]
    for g in range(1, grps):
        total = total + grp_sums[g]

    row_sums[pl.ds(me, 1)] = total[None]
    last_copies = to_rows(row_sums.at[me], row_sums.at[me], send_row, recv_row)
    for copy in copies:
        copy.wait_send()
    for copy in last_copies:
        copy.wait()
    total = row_sums[0]
    for r in range(1, rows):
        total = total + row_sums[r]
    out_ref[...] = total * factor


def body(date_keys, product_keys, quantity, date_flags, category, unit_price, unit_cost):
    rows, grps = lax.axis_size("rows"), lax.axis_size("grp")
    facts = date_keys.shape[0]
    shard = unit_price.shape[0]
    flag_shard = date_flags.shape[0]
    table_rows = cdiv(cdiv(shard, LANES), 16) * 16
    fact_rows = cdiv(facts, 32 * LANES) * 32
    all_rows = cdiv(rows * table_rows, LANES) * LANES
    all_flag_rows = cdiv(rows * cdiv(flag_shard, LANES), 16) * 16
    hi_cats = cdiv(CATS, LANES)
    size = 2 * hi_cats
    factor = CATS / (facts * rows * grps)

    def by_rows(array):
        return jnp.pad(array, (0, fact_rows * LANES - facts)).reshape(fact_rows, LANES)

    f32, i32 = jnp.float32, jnp.int32
    dense = (fact_rows, LANES)
    scratch = [
        ((rows, 1, flag_shard), i32),
        ((all_flag_rows, LANES), f32),
        ((1, shard), i32),
        ((1, shard), f32),
        ((1, shard), f32),
        ((rows, 3 * table_rows, LANES), f32),
        (dense, i32),
        (dense, i32),
        (dense, f32),
        (dense, f32),
        (dense, f32),
        (dense, i32),
        (dense, f32),
        (dense, f32),
        (dense, f32),
        ((SPLITS,) + dense, f32),
        ((all_rows, LANES), f32),
        ((2 * SPLITS, all_rows, LANES), f32),
        ((all_rows, LANES), f32),
        ((all_rows, LANES), f32),
        ((grps, size, LANES), f32),
        ((rows, size, LANES), f32),
    ]
    out = pl.pallas_call(
        functools.partial(kernel, rows, grps, factor),
        out_shape=jax.ShapeDtypeStruct((size, LANES), f32),
        in_specs=[pl.BlockSpec(memory_space=pltpu.HBM)] * 7,
        out_specs=pl.BlockSpec(memory_space=pltpu.VMEM),
        scratch_shapes=[pltpu.VMEM(shape, kind) for shape, kind in scratch]
        + [pltpu.SemaphoreType.DMA((7,))]
        + [pltpu.SemaphoreType.DMA((rows,))] * 4
        + [pltpu.SemaphoreType.DMA((grps,))] * 2
        + [pltpu.SemaphoreType.DMA((rows,))] * 2,
        compiler_params=pltpu.CompilerParams(
            collective_id=0,
            has_side_effects=True,
        ),
    )(
        date_flags,
        category.reshape(1, -1),
        unit_price.reshape(1, -1),
        unit_cost.reshape(1, -1),
        by_rows(date_keys),
        by_rows(product_keys),
        by_rows(quantity),
    )
    return (
        out[:hi_cats].reshape(-1)[:CATS],
        out[hi_cats:].reshape(-1)[:CATS],
    )


def solution(mesh):
    return jax.shard_map(
        body,
        mesh=mesh,
        in_specs=(
            P(("rows", "grp")),
            P(("rows", "grp")),
            P(("rows", "grp")),
            P("rows"),
            P("rows"),
            P("rows"),
            P("rows"),
        ),
        out_specs=(P(), P()),
        check_vma=False,
    )
```
